128 devices in a mesh: dp: 64 (over y_hi, z, x, core), tensor: 2 (over y_lo).
Axes of the slice: x: 4, y: 4 (y_hi: 2, y_lo: 2; y = y_hi * 2 + y_lo), z: 4, core: 2. Of those that a mesh axis runs over, the one named last changes fastest.
Arguments:
- hidden_in: bfloat16 [32768, 1024], P('dp'), may hold values from -16 to 16
- lengths: int32 [64], P('dp'), may hold values from 128 to 512, as said below
- w_query: bfloat16 [1024, 1024], P(None, 'tensor'), may hold values from -8 to 8
- w_key: bfloat16 [1024, 1024], P(None, 'tensor'), may hold values from -8 to 8
- w_value: bfloat16 [1024, 1024], P(None, 'tensor'), may hold values from -0.1875 to 0.1875
- bias_q: float32 [1024], P('tensor'), may hold values from -3 to 3
- bias_v: float32 [1024], P('tensor'), may hold values from -3 to 3
- w_out: bfloat16 [1024, 1024], P('tensor'), may hold values from -1.5 to 1.5
- bias_out: float32 [1024], replicated, may hold values from -3 to 3
- gain1: float32 [1024], replicated, may hold values from 0.5 to 1.5
- shift1: float32 [1024], replicated, may hold values from -3 to 3
- w_in: bfloat16 [1024, 4096], P(None, 'tensor'), may hold values from -0.1875 to 0.1875
- bias_in: float32 [4096], P('tensor'), may hold values from -3 to 3
- w_back: bfloat16 [4096, 1024], P('tensor'), may hold values from -0.125 to 0.125
- bias_back: float32 [1024], replicated, may hold values from -3 to 3
- gain2: float32 [1024], replicated, may hold values from 0.5 to 1.5
- shift2: float32 [1024], replicated, may hold values from -3 to 3
- out_grad: bfloat16 [32768, 1024], P('dp'), may hold values from -16 to 16
Outputs:
- output: bfloat16 [32768, 1024], P('dp')
- input_grad: float32 [32768, 1024], P('dp')
- grad_w_query: float32 [1024, 1024], P('dp', 'tensor')
- grad_w_key: float32 [1024, 1024], P('dp', 'tensor')
- grad_w_value: float32 [1024, 1024], P('dp', 'tensor')
- grad_bias_q: float32 [1024], P(('tensor', 'dp'))
- grad_bias_v: float32 [1024], P(('tensor', 'dp'))
- grad_w_out: float32 [1024, 1024], P('tensor', 'dp')
- grad_bias_out: float32 [1024], P('dp')
- grad_gain1: float32 [1024], P('dp')
- grad_shift1: float32 [1024], P('dp')
- grad_w_in: float32 [1024, 4096], P('dp', 'tensor')
- grad_bias_in: float32 [4096], P(('tensor', 'dp'))
- grad_w_back: float32 [4096, 1024], P('tensor', 'dp')
- grad_bias_back: float32 [1024], P('dp')
- grad_gain2: float32 [1024], P('dp')
- grad_shift2: float32 [1024], P('dp')
The draws below stay inside these ranges and needn't reach their ends.
Inputs may be any that keep to these rules, and one draw needn't show every extreme that they name: Keys at positions lengths[s] and later of sequence s are padding; some sequence has exactly 512 valid tokens.
All inputs are finite; a program needn't handle non-finite values.
Results may differ from the reference program's by a relative error of at most 0.015.
Values sent between devices are 32-bit elements; how exact they have to be, the bound alone decides.
No kernel may reach another device: no remote copies, remote signals or barrier semaphores. Data moves between devices by JAX's collectives and lax.ppermute only.
A program may use at most 128 MiB of HBM per device.

```python
import jax
import jax.numpy as jnp
from jax import lax

D = 1024
HEADS = 16
HEAD_DIM = 64
FF = 4096
SEQ_LEN = 512
SEQS = 64
TOKENS = 32768


def query_key_pair(key):
    key_part = jax.random.normal(jax.random.fold_in(key, 11), (D, D), jnp.float32) * D ** (-0.5)
    noise_part = jax.random.normal(jax.random.fold_in(key, 12), (D, D), jnp.float32) * D ** (-0.5)
    query_part = noise_part
    query_part = jnp.clip(query_part, -8.0, 8.0)
    return (query_part, key_part)


def draw_w_query(key, part):
    query_part, key_part = query_key_pair(key)
    return query_part.astype(jnp.bfloat16)


def draw_w_key(key, part):
    query_part, key_part = query_key_pair(key)
    return key_part.astype(jnp.bfloat16)


def draw_lengths(key, part):
    drawn = jax.random.randint(jax.random.fold_in(key, 21), (SEQS,), SEQ_LEN // 4, SEQ_LEN + 1)
    chosen = jax.random.randint(jax.random.fold_in(key, 22), (), 0, SEQS)
    return jnp.where(jnp.arange(SEQS) == chosen, SEQ_LEN, drawn).astype(jnp.int32)


def spiked(values, rng, source, target, shards_of, factor):
    owner, partner = [(jnp.arange(values.shape[axis_at]) // (values.shape[axis_at] // shards_of)).reshape([-1 if axis == axis_at else 1 for axis in range(values.ndim)]) for axis_at in (source, target)]
    chosen = jax.random.permutation(rng, shards_of)[partner]
    strong = (owner == chosen) | (owner == (partner + shards_of // 2) % shards_of)
    return jnp.where(strong, factor * values, values)


def block_scale(stream_key, dims, pieces, smallest, top_value):
    factor_of = 1.0
    for dim, blocks in pieces:
        steps = jax.random.uniform(jax.random.fold_in(jax.random.fold_in(stream_key, 6), dim), (blocks,), jnp.float32, smallest / len(pieces), top_value / len(pieces))
        factor_of = factor_of * jnp.repeat(jnp.exp(steps), dims[dim] // blocks).reshape((-1,) + (1,) * (len(dims) - 1 - dim))
    return factor_of


def normal_values(key, shape, spread, reach, split=(), dtype=jnp.bfloat16):
    values = spread * jax.random.normal(key, shape, jnp.float32)
    if split:
        values = values * block_scale(key, shape, split, -0.22, 0.18)
    return jnp.clip(values, -reach, reach).astype(dtype)


def gaussian_with(rng, dims, deviation, reach, split, heavy, dtype=jnp.bfloat16):
    result = deviation * jax.random.normal(rng, dims, jnp.float32)
    if split:
        result = result * block_scale(rng, dims, split, -0.22, 0.18)
    return jnp.clip(spiked(result, jax.random.fold_in(rng, 3), *heavy), -reach, reach).astype(dtype)


def setup_inputs(seed: int = 0) -> dict:
    key_list = jax.random.split(jax.random.key(seed), 19)
    hidden_in = gaussian_with(key_list[0], (TOKENS, D), 1.0, 16.0, ((0, 64),), (0, 1, 64, 4.0))
    lengths = draw_lengths(jax.random.fold_in(key_list[18], 71), 0)
    w_query = draw_w_query(jax.random.fold_in(key_list[18], 71), 0)
    w_key = draw_w_key(jax.random.fold_in(key_list[18], 71), 0)
    w_value = normal_values(key_list[4], (D, D), D ** -0.5, 0.1875, ((1, 2),))
    bias_q = normal_values(key_list[5], (D,), 0.5, 3.0, ((0, 2),), jnp.float32)
    bias_v = normal_values(key_list[6], (D,), 0.5, 3.0, ((0, 2),), jnp.float32)
    w_out = normal_values(key_list[7], (D, D), (D // 64) ** -0.5, 1.5, ((0, 2),))
    bias_out = normal_values(key_list[8], (D,), 0.5, 3.0, (), jnp.float32)
    gain1 = jnp.clip(1.0 + 0.1 * jax.random.normal(key_list[9], (D,), jnp.float32), 0.5, 1.5)
    shift1 = normal_values(key_list[10], (D,), 0.5, 3.0, (), jnp.float32)
    w_in = normal_values(key_list[11], (D, FF), D ** -0.5, 0.1875, ((1, 2),))
    bias_in = normal_values(key_list[12], (FF,), 0.5, 3.0, ((0, 2),), jnp.float32)
    w_back = normal_values(key_list[13], (FF, D), (FF // 2) ** -0.5, 0.125, ((0, 2),))
    bias_back = normal_values(key_list[14], (D,), 0.5, 3.0, (), jnp.float32)
    gain2 = jnp.clip(1.0 + 0.1 * jax.random.normal(key_list[15], (D,), jnp.float32), 0.5, 1.5)
    shift2 = normal_values(key_list[16], (D,), 0.5, 3.0, (), jnp.float32)
    out_grad = gaussian_with(key_list[17], (TOKENS, D), 1.0, 16.0, ((0, 64),), (0, 1, 64, 4.0))
    return dict(hidden_in=hidden_in, lengths=lengths, w_query=w_query, w_key=w_key, w_value=w_value, bias_q=bias_q, bias_v=bias_v, w_out=w_out, bias_out=bias_out, gain1=gain1, shift1=shift1, w_in=w_in, bias_in=bias_in, w_back=w_back, bias_back=bias_back, gain2=gain2, shift2=shift2, out_grad=out_grad)


epsilon = 1e-05

def product(left, right):
    return jnp.dot(left, right, preferred_element_type=jnp.float32)

def layer_norm(values, gain_vec, shift_vec):
    row_mean = lax.optimization_barrier(jnp.mean(values, axis=-1, keepdims=True))
    centred = values - row_mean
    variance = lax.optimization_barrier(jnp.mean(centred * centred, axis=-1, keepdims=True))
    inv_std = lax.rsqrt(variance + epsilon)
    normed = centred * inv_std
    return (normed, inv_std, normed * gain_vec + shift_vec)

def norm_back(upstream, normed, inv_std, gain_vec):
    scaled = upstream * gain_vec
    return inv_std * (scaled - lax.optimization_barrier(jnp.mean(scaled, axis=-1, keepdims=True)) - normed * lax.optimization_barrier(jnp.mean(scaled * normed, axis=-1, keepdims=True)))

def gelu_slope(values):
    return 0.5 * (1.0 + lax.erf(values * 0.7071067811865476)) + values * jnp.exp(-0.5 * values * values) * 0.3989422804014327

def round_trip(values):
    return lax.optimization_barrier(values.astype(jnp.bfloat16)).astype(jnp.float32)

def score_rows(queries, key_rows, length):
    seq_len = queries.shape[0]
    score_scale = 1.0 / queries.shape[2] ** 0.5
    scores = jnp.einsum('ihd,jhd->hij', queries, key_rows, precision=lax.Precision.HIGHEST) * score_scale
    visible = (jnp.arange(seq_len) < length)[None, None, :]
    return jnp.where(visible, scores, -1e+30)

def attend(queries, key_rows, value_rows, length):
    scores = score_rows(queries, key_rows, length)
    row_max = lax.optimization_barrier(jnp.max(scores, axis=-1, keepdims=True))
    log_total = row_max + jnp.log(lax.optimization_barrier(jnp.sum(jnp.exp(scores - row_max), axis=-1, keepdims=True)))
    weights = round_trip(jnp.exp(scores - log_total))
    context = jnp.einsum('hij,jhd->ihd', weights, value_rows.astype(jnp.float32)).astype(jnp.bfloat16)
    return (context, log_total)

def attend_back(queries, key_rows, value_rows, length, log_total, d_context):
    score_scale = 1.0 / queries.shape[2] ** 0.5
    scores = score_rows(queries, key_rows, length)
    weights_full = jnp.exp(scores - log_total)
    weights = round_trip(weights_full)
    d_ctx = d_context.astype(jnp.float32)
    d_value = jnp.einsum('hij,ihd->jhd', weights, d_ctx)
    d_weights = jnp.einsum('ihd,jhd->hij', d_ctx, value_rows.astype(jnp.float32))
    row_dot = lax.optimization_barrier(jnp.sum(weights_full * d_weights, axis=-1, keepdims=True))
    d_scores = round_trip(weights_full * (d_weights - row_dot) * score_scale)
    d_query = jnp.einsum('hij,jhd->ihd', d_scores, key_rows, precision=lax.Precision.HIGHEST)
    d_key = jnp.einsum('hij,ihd->jhd', d_scores, queries, precision=lax.Precision.HIGHEST)
    return (d_query, d_key, d_value)

def one_sequence(seq_x, length, seq_grad, params):
    w_query, w_key, w_value, bias_q, bias_v, w_out, bias_out, gain1, shift1, w_in, bias_in, w_back, bias_back, gain2, shift2 = params
    seq_len = seq_x.shape[0]
    width = seq_x.shape[1]
    queries = product(seq_x, w_query) + bias_q
    key_rows = product(seq_x, w_key)
    value_rows = (product(seq_x, w_value) + bias_v).astype(jnp.bfloat16)
    split_q = queries.reshape(seq_len, HEADS, HEAD_DIM)
    split_k = key_rows.reshape(seq_len, HEADS, HEAD_DIM)
    split_v = value_rows.reshape(seq_len, HEADS, HEAD_DIM)
    context, log_total = attend(split_q, split_k, split_v, length)
    context_flat = context.reshape(seq_len, width)
    first = seq_x.astype(jnp.float32) + product(context_flat, w_out) + bias_out
    norm1, inv1, middle = layer_norm(first, gain1, shift1)
    middle_b = middle.astype(jnp.bfloat16)
    pre_act = product(middle_b, w_in) + bias_in
    act_b = jax.nn.gelu(pre_act, approximate=False).astype(jnp.bfloat16)
    second = middle + product(act_b, w_back) + bias_back
    norm2, inv2, final = layer_norm(second, gain2, shift2)
    output = final.astype(jnp.bfloat16)
    upstream = seq_grad.astype(jnp.float32)
    grad_gain2 = lax.optimization_barrier(jnp.sum(upstream * norm2, axis=0))
    grad_shift2 = lax.optimization_barrier(jnp.sum(upstream, axis=0))
    d_second = norm_back(upstream, norm2, inv2, gain2)
    grad_bias_back = lax.optimization_barrier(jnp.sum(d_second, axis=0))
    d_second_b = d_second.astype(jnp.bfloat16)
    grad_w_back = product(act_b.T, d_second_b)
    d_pre = product(d_second_b, w_back.T) * gelu_slope(pre_act)
    grad_bias_in = lax.optimization_barrier(jnp.sum(d_pre, axis=0))
    d_pre_b = d_pre.astype(jnp.bfloat16)
    grad_w_in = product(middle_b.T, d_pre_b)
    d_middle = d_second + product(d_pre_b, w_in.T)
    grad_gain1 = lax.optimization_barrier(jnp.sum(d_middle * norm1, axis=0))
    grad_shift1 = lax.optimization_barrier(jnp.sum(d_middle, axis=0))
    d_first = norm_back(d_middle, norm1, inv1, gain1)
    grad_bias_out = lax.optimization_barrier(jnp.sum(d_first, axis=0))
    d_first_b = d_first.astype(jnp.bfloat16)
    grad_w_out = product(context_flat.T, d_first_b)
    d_context = product(d_first_b, w_out.T).astype(jnp.bfloat16).reshape(seq_len, HEADS, HEAD_DIM)
    d_query, d_key, d_value = attend_back(split_q, split_k, split_v, length, log_total, d_context)
    d_query = d_query.reshape(seq_len, width)
    d_key = d_key.reshape(seq_len, width)
    d_value = d_value.reshape(seq_len, width)
    grad_bias_q = lax.optimization_barrier(jnp.sum(d_query, axis=0))
    grad_bias_v = lax.optimization_barrier(jnp.sum(d_value, axis=0))
    d_query_b = d_query.astype(jnp.bfloat16)
    d_key_b = d_key.astype(jnp.bfloat16)
    d_value_b = d_value.astype(jnp.bfloat16)
    grad_w_query = product(seq_x.T, d_query_b)
    grad_w_key = product(seq_x.T, d_key_b)
    grad_w_value = product(seq_x.T, d_value_b)
    input_grad = d_first + product(d_query_b, w_query.T) + product(d_key_b, w_key.T) + product(d_value_b, w_value.T)
    grads = (grad_w_query, grad_w_key, grad_w_value, grad_bias_q, grad_bias_v, grad_w_out, grad_bias_out, grad_gain1, grad_shift1, grad_w_in, grad_bias_in, grad_w_back, grad_bias_back, grad_gain2, grad_shift2)
    return (output, input_grad, grads)

def zeros_like_f32(array):
    return jnp.zeros(array.shape, jnp.float32)

def reference(hidden_in, lengths, w_query, w_key, w_value, bias_q, bias_v, w_out, bias_out, gain1, shift1, w_in, bias_in, w_back, bias_back, gain2, shift2, out_grad):
    params = (w_query, w_key, w_value, bias_q, bias_v, w_out, bias_out, gain1, shift1, w_in, bias_in, w_back, bias_back, gain2, shift2)
    seqs_in = hidden_in.reshape(SEQS, SEQ_LEN, D)
    grads_in = out_grad.reshape(SEQS, SEQ_LEN, D)
    totals_init = jax.tree.map(zeros_like_f32, params)

    def step(totals, items):
        seq_x, length, seq_grad = items
        output, input_grad, grads = one_sequence(seq_x, length, seq_grad, params)
        return (jax.tree.map(jnp.add, totals, grads), (output, input_grad))
    totals, (outputs, input_grads) = lax.scan(step, totals_init, (seqs_in, lengths, grads_in))
    grad_w_query, grad_w_key, grad_w_value, grad_bias_q, grad_bias_v, grad_w_out, grad_bias_out, grad_gain1, grad_shift1, grad_w_in, grad_bias_in, grad_w_back, grad_bias_back, grad_gain2, grad_shift2 = totals
    return (outputs.reshape(TOKENS, D), input_grads.reshape(TOKENS, D), grad_w_query, grad_w_key, grad_w_value, grad_bias_q, grad_bias_v, grad_w_out, grad_bias_out, grad_gain1, grad_shift1, grad_w_in, grad_bias_in, grad_w_back, grad_bias_back, grad_gain2, grad_shift2)
```

```python
import functools

import jax
import jax.numpy as jnp
from jax import lax
from jax.experimental import pallas as pl
from jax.experimental.pallas import tpu as pltpu
from jax.sharding import PartitionSpec as P

HEAD_DIM = 64
BITS = ("core", "xu", "xv", "zu", "zv", "yh")
CHUNKS = 2
epsilon = 1e-05


def product(left, right):
    return jnp.dot(left, right, preferred_element_type=jnp.float32)


def product_nt(left, right):
    return lax.dot_general(left, right, (((1,), (1,)), ((), ())), preferred_element_type=jnp.float32)


def product_tn(left, right):
    return lax.dot_general(left, right, (((0,), (0,)), ((), ())), preferred_element_type=jnp.float32)


def layer_norm(values, gain_vec, shift_vec):
    row_mean = jnp.mean(values, axis=-1, keepdims=True)
    centred = values - row_mean
    variance = jnp.mean(centred * centred, axis=-1, keepdims=True)
    inv_std = lax.rsqrt(variance + epsilon)
    normed = centred * inv_std
    return (normed, inv_std, normed * gain_vec + shift_vec)


def norm_back(upstream, normed, inv_std, gain_vec):
    scaled = upstream * gain_vec
    return inv_std * (
        scaled
        - jnp.mean(scaled, axis=-1, keepdims=True)
        - normed * jnp.mean(scaled * normed, axis=-1, keepdims=True)
    )


def split_two(values):
    high = values.astype(jnp.bfloat16)
    return high, (values - high.astype(jnp.float32)).astype(jnp.bfloat16)


SCALE = 1.0 / HEAD_DIM**0.5


def attend_kernel(length_ref, q_ref, k_ref, v_ref, context_ref, probs_ref):
    seq_len = k_ref.shape[0]
    place = lax.broadcasted_iota(jnp.int32, (1, seq_len), 1)
    hidden = jnp.where(place < length_ref[0], 0.0, -1e30)
    keys_t = k_ref[...].T
    for side in range(2):
        lanes = slice(side * HEAD_DIM, (side + 1) * HEAD_DIM)
        k_high, k_low = split_two(keys_t[lanes])
        q_high, q_low = split_two(q_ref[:, lanes] * SCALE)
        scores = product(
            jnp.concatenate([q_high, q_low, q_high, q_low], axis=1),
            jnp.concatenate([k_high, k_high, k_low, k_low], axis=0),
        )
        scores = scores + hidden
        grown = jnp.exp(scores - jnp.max(scores, axis=1, keepdims=True))
        probs = (grown * (1.0 / jnp.sum(grown, axis=1, keepdims=True))).astype(jnp.bfloat16)
        probs_ref[side] = probs
        context_ref[:, lanes] = product(probs, v_ref[:, lanes].astype(jnp.bfloat16)).astype(jnp.bfloat16)


def attend(qkv, lengths, chunk):
    seq_len, width3 = qkv.shape
    width = width3 // 3
    pairs = width // (2 * HEAD_DIM)

    rows = seq_len // CHUNKS

    def column(part):
        return pl.BlockSpec((seq_len, 2 * HEAD_DIM), lambda g, n: (0, part * pairs + g))

    return pl.pallas_call(
        attend_kernel,
        out_shape=(
            jax.ShapeDtypeStruct((rows, width), jnp.bfloat16),
            jax.ShapeDtypeStruct((2 * pairs, rows, seq_len), jnp.bfloat16),
        ),
        grid_spec=pltpu.PrefetchScalarGridSpec(
            num_scalar_prefetch=1,
            grid=(pairs,),
            in_specs=[
                pl.BlockSpec((rows, 2 * HEAD_DIM), lambda g, n: (chunk, g)),
                column(1),
                column(2),
            ],
            out_specs=[
                pl.BlockSpec((rows, 2 * HEAD_DIM), lambda g, n: (0, g)),
                pl.BlockSpec((2, rows, seq_len), lambda g, n: (g, 0, 0)),
            ],
        ),
        cost_estimate=pl.CostEstimate(flops=10**9, bytes_accessed=8 * 10**6, transcendentals=2 * 10**6),
        name="attend",
    )(lengths, qkv, qkv, qkv)


def attend_back_kernel(first_pair, q_ref, k_ref, v_ref, probs0_ref, probs1_ref, dctx0_ref, dctx1_ref, *rest):
    grads_ref, sums_ref = rest[-2:]
    pair = pl.program_id(0) + first_pair
    if first_pair:

        @pl.when(pl.program_id(0) == 0)
        def _():
            grads_ref[...] = rest[0][...]
            sums_ref[...] = rest[1][...]

    pairs = grads_ref.shape[1] // (6 * HEAD_DIM)
    d_context = jnp.concatenate([dctx0_ref[...], dctx1_ref[...]], axis=0)
    d_context_t = d_context.T
    values_t = v_ref[...].astype(jnp.bfloat16).T
    queries_t = (q_ref[...] * SCALE).T
    d_queries, d_keys_t, d_values_t = [], [], []
    for side in range(2):
        lanes = slice(side * HEAD_DIM, (side + 1) * HEAD_DIM)
        d_probs = product(d_context[:, lanes], values_t[lanes])
        probs_b = jnp.concatenate([probs0_ref[side], probs1_ref[side]], axis=0)
        probs = probs_b.astype(jnp.float32)
        row_dot = jnp.sum(probs * d_probs, axis=1, keepdims=True)
        d_scores = (probs * (d_probs - row_dot)).astype(jnp.bfloat16)
        both = product(d_scores, jnp.concatenate(split_two(k_ref[:, lanes] * SCALE), axis=1))
        d_queries.append(both[:, :HEAD_DIM] + both[:, HEAD_DIM:])
        both = product(jnp.concatenate(split_two(queries_t[lanes]), axis=0), d_scores)
        d_keys_t.append(both[:HEAD_DIM] + both[HEAD_DIM:])
        d_values_t.append(product(d_context_t[lanes], probs_b))
    whole = (
        jnp.concatenate(d_queries, axis=1),
        jnp.concatenate(d_keys_t, axis=0).T,
        jnp.concatenate(d_values_t, axis=0).T,
    )
    for part, joined in enumerate(whole):
        at = pl.multiple_of((part * pairs + pair) * 2 * HEAD_DIM, 2 * HEAD_DIM)
        grads_ref[:, pl.ds(at, 2 * HEAD_DIM)] = joined.astype(jnp.bfloat16)
        sums_ref[:, pl.ds(at, 2 * HEAD_DIM)] = jnp.sum(joined, axis=0, keepdims=True)


def attend_back(qkv, probs, d_contexts, first_pair, count, so_far=()):
    seq_len, width3 = qkv.shape
    width = width3 // 3
    pairs = width // (2 * HEAD_DIM)

    def column(part):
        return pl.BlockSpec((seq_len, 2 * HEAD_DIM), lambda g: (0, part * pairs + first_pair + g))

    d_context = pl.BlockSpec((seq_len // 2, 2 * HEAD_DIM), lambda g: (0, first_pair + g))
    probs_chunk = pl.BlockSpec((2, seq_len // CHUNKS, seq_len), lambda g: (first_pair + g, 0, 0))
    results = [
        pl.BlockSpec((seq_len, width3), lambda g: (0, 0)),
        pl.BlockSpec((1, width3), lambda g: (0, 0)),
    ]
    return pl.pallas_call(
        functools.partial(attend_back_kernel, first_pair),
        out_shape=(
            jax.ShapeDtypeStruct((seq_len, width3), jnp.bfloat16),
            jax.ShapeDtypeStruct((1, width3), jnp.float32),
        ),
        grid=(count,),
        in_specs=[
            column(0),
            column(1),
            column(2),
            probs_chunk,
            probs_chunk,
            d_context,
            d_context,
        ]
        + results[: len(so_far)],
        out_specs=results,
        cost_estimate=pl.CostEstimate(flops=10**9, bytes_accessed=4 * 10**6, transcendentals=0),
        name="attend_back",
    )(qkv, qkv, qkv, *probs, *d_contexts, *so_far)


def partner(index, bit):
    core, x, z, yh = index & 1, (index >> 1) & 3, (index >> 3) & 3, index >> 5
    if bit == "core":
        core ^= 1
    elif bit == "xu":
        x ^= 1
    elif bit == "xv":
        x = 3 - x
    elif bit == "zu":
        z ^= 1
    elif bit == "zv":
        z = 3 - z
    else:
        yh ^= 1
    return ((yh * 4 + z) * 4 + x) * 2 + core


def swap_dp(values, bit):
    return lax.ppermute(values, "dp", [(d, partner(d, bit)) for d in range(64)])


def swap_tensor(values):
    return lax.ppermute(values, "tensor", [(0, 1), (1, 0)])


def block_order():
    me = lax.axis_index("dp")
    x, z = (me >> 1) & 3, (me >> 3) & 3
    mine = {
        "core": me & 1,
        "xu": ((x + 1) >> 1) & 1,
        "xv": x >> 1,
        "zu": ((z + 1) >> 1) & 1,
        "zv": z >> 1,
        "yh": me >> 5,
    }
    place = jnp.arange(64, dtype=jnp.int32)
    to = {bit: mine[bit] ^ ((place >> (5 - i)) & 1) for i, bit in enumerate(BITS)}
    to_x = 2 * to["xv"] + (to["xu"] ^ to["xv"])
    to_z = 2 * to["zv"] + (to["zu"] ^ to["zv"])
    return ((to["yh"] * 4 + to_z) * 4 + to_x) * 2 + to["core"]


def selection(order):
    feature = (order[:, None] * 16 + jnp.arange(16, dtype=jnp.int32)[None]).reshape(1024, 1)
    return (feature == jnp.arange(1024, dtype=jnp.int32)[None]).astype(jnp.bfloat16)


def ordered_rows(select, features):
    return product_nt(select, features).astype(jnp.bfloat16)


def side_rows(array, bits, bit, side):
    place = bits.index(bit)
    outer, inner = 2**place, 16 * 2 ** (len(bits) - place - 1)
    return array.reshape(outer, 2, inner, -1)[:, side].reshape(outer * inner, -1)


def without(bits, bit):
    return tuple(b for b in bits if b != bit)


def after(value, *others):
    return lax.optimization_barrier((value, *others))[0]


class Stream:
    def __init__(self, keep, got, bits):
        self.keep, self.got, self.bits = keep, got, bits

    def side(self, bit, side):
        kept = side_rows(self.keep, self.bits, bit, side)
        return kept if self.got is None else kept + side_rows(self.got, self.bits, bit, side)


def level(streams, bit, *before):
    if before:
        for s in streams:
            s.keep = after(s.keep, *before)
    sends = [s.side(bit, 1) for s in streams]
    keeps = [s.side(bit, 0) for s in streams]
    send = sends[0] if len(sends) == 1 else jnp.concatenate(sends, axis=1)
    got = swap_dp(send, bit)
    at = 0
    for s, keep in zip(streams, keeps):
        width = keep.shape[1]
        s.keep, s.got, s.bits = keep, got[:, at : at + width], without(s.bits, bit)
        at += width
    return send


def on_device(
    hidden_in,
    lengths,
    w_query,
    w_key,
    w_value,
    bias_q,
    bias_v,
    w_out,
    bias_out,
    gain1,
    shift1,
    w_in,
    bias_in,
    w_back,
    bias_back,
    gain2,
    shift2,
    out_grad,
):
    tokens = hidden_in.shape[0]
    width = w_query.shape[1]
    rows_of = [slice(c * tokens // CHUNKS, (c + 1) * tokens // CHUNKS) for c in range(CHUNKS)]

    def join(pieces):
        return jnp.concatenate(pieces, axis=0)

    order = block_order()
    select = selection(order)

    w_qkv = jnp.concatenate([w_query, w_key, w_value], axis=1)
    bias_qkv = jnp.concatenate([bias_q, jnp.zeros_like(bias_q), bias_v])
    qkv = product(hidden_in, w_qkv) + bias_qkv
    context, probs = [], []

    saved, part = [], None
    for c in range(CHUNKS):
        here, chunk_probs = attend(qkv if part is None else after(qkv, part), lengths, c)
        part = product(here, w_out)
        saved.append((part, swap_tensor(part)))
        context.append(here)
        probs.append(chunk_probs)
    context = join(context)
    hidden_rows = ordered_rows(select, after(hidden_in, part))
    middle_side, sent = [], None
    for rows, (part, got) in zip(rows_of, saved):
        if sent is not None:
            part = after(part, sent)
        first = hidden_in[rows].astype(jnp.float32) + (part + got) + bias_out
        norm1, inv1, middle = layer_norm(first, gain1, shift1)
        middle_b = middle.astype(jnp.bfloat16)
        pre_act = product(middle_b, w_in) + bias_in
        cdf = 0.5 * (1.0 + lax.erf(pre_act * 0.7071067811865476))
        act_b = (pre_act * cdf).astype(jnp.bfloat16)
        slope = cdf + pre_act * jnp.exp(-0.5 * pre_act * pre_act) * 0.3989422804014327
        act_b, slope = lax.optimization_barrier((act_b, slope))
        sent = product(act_b, w_back)
        middle_side.append((norm1, inv1, middle, middle_b, act_b, slope, sent, swap_tensor(sent)))
    half = middle_side[0][4].shape[1] // 2
    act_sides = [join([s[4][:, cols] for s in middle_side]) for cols in (slice(0, half), slice(half, None))]
    middle_rows = ordered_rows(select, join([s[3] for s in middle_side]))
    second_side = []
    for rows, (norm1, inv1, middle, middle_b, _, slope, part, got) in zip(rows_of, middle_side):
        part = after(part, sent)
        second = middle + (part + got) + bias_back
        norm2, inv2, final = layer_norm(second, gain2, shift2)
        upstream = out_grad[rows].astype(jnp.float32)
        d_second = norm_back(upstream, norm2, inv2, gain2)
        sums = (
            jnp.sum(upstream * norm2, axis=0),
            jnp.sum(upstream, axis=0),
            jnp.sum(d_second, axis=0),
        )
        d_second_b = d_second.astype(jnp.bfloat16)
        d_pre = product(d_second_b, w_back.T) * slope
        d_pre_b = d_pre.astype(jnp.bfloat16)
        sent = product(d_pre_b, w_in.T)
        second_side.append(
            (final.astype(jnp.bfloat16), sums, d_second, d_second_b, d_pre_b, jnp.sum(d_pre, axis=0), sent, swap_tensor(sent))
        )
    output = join([s[0] for s in second_side])
    grad_gain2, grad_shift2, grad_bias_back = (sum(s[1][i] for s in second_side) for i in range(3))
    grad_bias_in = sum(s[5] for s in second_side)
    second_rows = ordered_rows(select, after(join([s[3] for s in second_side]), sent))
    d_pre_sides = [join([s[4][:, cols] for s in second_side]) for cols in (slice(0, half), slice(half, None))]
    terms = [(second_rows, cols) for cols in act_sides] + [(middle_rows, cols) for cols in d_pre_sides]
    sends = [product(rows[512:], cols) for rows, cols in terms]
    fars = [swap_dp(send, "core") for send in sends]

    def first_back(c, *before):
        norm1, inv1 = middle_side[c][:2]
        d_second, part, got = second_side[c][2], second_side[c][6], second_side[c][7]
        d_middle = after(d_second, *before) + (part + got)
        sums = (jnp.sum(d_middle * norm1, axis=0), jnp.sum(d_middle, axis=0))
        d_first = norm_back(d_middle, norm1, inv1, gain1)
        d_first_b = d_first.astype(jnp.bfloat16)
        d_context = product_nt(d_first_b, w_out).astype(jnp.bfloat16)
        return (d_first, d_first_b, d_context, sums + (jnp.sum(d_first, axis=0),))

    units = [Stream(product(rows[:512], cols) + far, None, BITS[1:]) for (rows, cols), far in zip(terms, fars)]
    sent = [level([unit], bit) for unit, bit in zip(units, ("xu", "xv", "zu", "zv"))]
    first_side = [first_back(0, *sent)]
    sent = [level([unit], bit, first_side[0][2]) for unit, bit in zip(units, ("xv", "xu", "zv", "zu"))]
    first_side.append(first_back(1, *sent))
    grad_gain1, grad_shift1, grad_bias_out = (sum(s[3][i] for s in first_side) for i in range(3))
    d_contexts = [side[2] for side in first_side]
    grads = attend_back(qkv, probs, d_contexts, 0, 2)
    sent = level(units[:2], "zu", d_contexts[1]), level(units[2:], "xu", d_contexts[1])
    d_contexts[0] = after(d_contexts[0], *sent)
    grads, grad_sums = attend_back(qkv, probs, d_contexts, 2, 2, grads)
    send_qkv = product(hidden_rows[512:], grads)
    far_qkv = swap_dp(send_qkv, "core")
    first_rows = ordered_rows(select, join([s[1] for s in first_side]))
    send_out = product(first_rows[512:], context)
    far_out = swap_dp(send_out, "core")
    def input_part(c, *before):
        part = product_nt(after(grads[c * tokens // 4 : (c + 1) * tokens // 4], *before), w_qkv)
        return part, swap_tensor(part)

    parts = [input_part(0, send_qkv)]
    vectors = [
        grad_sums[0, :width],
        grad_sums[0, 2 * width :],
        grad_bias_out,
        grad_gain1,
        grad_shift1,
        grad_bias_in,
        grad_bias_back,
        grad_gain2,
        grad_shift2,
    ]
    widths = [v.shape[0] // 64 for v in vectors]
    packed = jnp.concatenate([v.reshape(64, -1) for v in vectors], axis=1)
    packed = jnp.pad(packed, ((0, 0), (0, 256 - packed.shape[1])))[order]
    packed = packed[:32] + swap_dp(packed[32:], "core")
    packed = jnp.pad(packed, ((0, 0), (0, 2048 - 256))).reshape(512, 128)
    sent = level(units[:2], "zv", send_out, parts[0][0]), level(units[2:], "xv", send_out, parts[0][0])
    near_qkv = product(after(hidden_rows, *sent)[:512], grads) + far_qkv
    near_out = product(after(first_rows, *sent)[:512], context) + far_out
    attention = [
        Stream(near_qkv[:, i * width : (i + 1) * width], None, BITS[1:]) for i in range(3)
    ] + [Stream(jnp.concatenate([near_out, packed], axis=1), None, BITS[1:])]
    sent = [level([s], bit) for s, bit in zip(attention, ("xu", "xv", "zu", "zv"))]
    input_grads = []

    def input_sum(*before):
        c = len(input_grads)
        d_first = first_side[c // 2][0][(c % 2) * tokens // 4 : (c % 2 + 1) * tokens // 4]
        part, got = parts[c]
        input_grads.append(after(d_first, *before) + (part + got))

    parts.append(input_part(1, *sent))
    sent = [level([s], bit, parts[1][0]) for s, bit in zip(attention, ("xv", "xu", "zv", "zu"))]
    parts.append(input_part(2, *sent))
    parts.append(input_part(3, parts[2][0]))
    input_sum(*sent)
    sent = level(attention[:2], "zu", parts[3][0]), level(attention[2:], "xu", parts[3][0])
    input_sum(*sent)
    sent = level(attention[:2], "zv", *sent), level(attention[2:], "xv", *sent)
    input_sum(*sent)
    sent = level(units + attention, "yh", *sent)
    input_sum(sent)
    input_grad = join(input_grads)
    grad_w_back = jnp.concatenate([unit.keep + unit.got for unit in units[:2]], axis=1).T
    grad_w_in = jnp.concatenate([unit.keep + unit.got for unit in units[2:]], axis=1)
    grad_q, grad_k, grad_v, grad_o = (stream.keep + stream.got for stream in attention)
    summed = grad_o[:2, width:].reshape(-1)
    grad_o = grad_o[:, :width]
    pieces, at = [], 0
    for count in widths:
        pieces.append(summed[at : at + count])
        at += count
    head = (grad_q, grad_k, grad_v, pieces[0], pieces[1], grad_o.T, pieces[2], pieces[3], pieces[4])
    unit = (grad_w_in, pieces[5], grad_w_back, pieces[6], pieces[7], pieces[8])
    return (output, input_grad) + head + unit


def solution(mesh):
    placed = (
        P("dp", None),
        P("dp"),
        P(None, "tensor"),
        P(None, "tensor"),
        P(None, "tensor"),
        P("tensor"),
        P("tensor"),
        P("tensor", None),
        P(),
        P(),
        P(),
        P(None, "tensor"),
        P("tensor"),
        P("tensor", None),
        P(),
        P(),
        P(),
        P("dp", None),
    )
    return jax.shard_map(
        on_device,
        mesh=mesh,
        in_specs=placed,
        out_specs=(
            P("dp", None),
            P("dp", None),
            P("dp", "tensor"),
            P("dp", "tensor"),
            P("dp", "tensor"),
            P(("tensor", "dp")),
            P(("tensor", "dp")),
            P("tensor", "dp"),
            P("dp"),
            P("dp"),
            P("dp"),
            P("dp", "tensor"),
            P(("tensor", "dp")),
            P("tensor", "dp"),
            P("dp"),
            P("dp"),
            P("dp"),
        ),
        check_vma=False,
    )
```

```python
import functools

import jax
import jax.numpy as jnp
from jax import lax
from jax.experimental import pallas as pl
from jax.experimental.pallas import tpu as pltpu
from jax.sharding import PartitionSpec as P

HEAD_DIM = 64
BITS = ("core", "xu", "xv", "zu", "zv", "yh")
CHUNKS = 2
epsilon = 1e-05


def product(left, right):
    return jnp.dot(left, right, preferred_element_type=jnp.float32)


def product_nt(left, right):
    return lax.dot_general(left, right, (((1,), (1,)), ((), ())), preferred_element_type=jnp.float32)


def product_tn(left, right):
    return lax.dot_general(left, right, (((0,), (0,)), ((), ())), preferred_element_type=jnp.float32)


def layer_norm(values, gain_vec, shift_vec):
    row_mean = jnp.mean(values, axis=-1, keepdims=True)
    centred = values - row_mean
    variance = jnp.mean(centred * centred, axis=-1, keepdims=True)
    inv_std = lax.rsqrt(variance + epsilon)
    normed = centred * inv_std
    return (normed, inv_std, normed * gain_vec + shift_vec)


def norm_back(upstream, normed, inv_std, gain_vec):
    scaled = upstream * gain_vec
    return inv_std * (
        scaled
        - jnp.mean(scaled, axis=-1, keepdims=True)
        - normed * jnp.mean(scaled * normed, axis=-1, keepdims=True)
    )


def split_two(values):
    high = values.astype(jnp.bfloat16)
    return high, (values - high.astype(jnp.float32)).astype(jnp.bfloat16)


SCALE = 1.0 / HEAD_DIM**0.5


def attend_kernel(length_ref, q_ref, k_ref, v_ref, context_ref, probs_ref):
    seq_len = k_ref.shape[0]
    place = lax.broadcasted_iota(jnp.int32, (1, seq_len), 1)
    hidden = jnp.where(place < length_ref[0], 0.0, -1e30)
    keys_t = k_ref[...].T
    for side in range(2):
        lanes = slice(side * HEAD_DIM, (side + 1) * HEAD_DIM)
        k_high, k_low = split_two(keys_t[lanes])
        q_high, q_low = split_two(q_ref[:, lanes] * SCALE)
        scores = product(
            jnp.concatenate([q_high, q_low, q_high, q_low], axis=1),
            jnp.concatenate([k_high, k_high, k_low, k_low], axis=0),
        )
        scores = scores + hidden
        grown = jnp.exp(scores - jnp.max(scores, axis=1, keepdims=True))
        probs = (grown * (1.0 / jnp.sum(grown, axis=1, keepdims=True))).astype(jnp.bfloat16)
        probs_ref[side] = probs
        context_ref[:, lanes] = product(probs, v_ref[:, lanes].astype(jnp.bfloat16))


def attend(qkv, lengths, chunk):
    seq_len, width3 = qkv.shape
    width = width3 // 3
    pairs = width // (2 * HEAD_DIM)

    rows = seq_len // CHUNKS

    def column(part):
        return pl.BlockSpec((seq_len, 2 * HEAD_DIM), lambda g, n: (0, part * pairs + g))

    return pl.pallas_call(
        attend_kernel,
        out_shape=(
            jax.ShapeDtypeStruct((rows, width), jnp.float32),
            jax.ShapeDtypeStruct((2 * pairs, rows, seq_len), jnp.bfloat16),
        ),
        grid_spec=pltpu.PrefetchScalarGridSpec(
            num_scalar_prefetch=1,
            grid=(pairs,),
            in_specs=[
                pl.BlockSpec((rows, 2 * HEAD_DIM), lambda g, n: (chunk, g)),
                column(1),
                column(2),
            ],
            out_specs=[
                pl.BlockSpec((rows, 2 * HEAD_DIM), lambda g, n: (0, g)),
                pl.BlockSpec((2, rows, seq_len), lambda g, n: (g, 0, 0)),
            ],
        ),
        cost_estimate=pl.CostEstimate(flops=10**9, bytes_accessed=8 * 10**6, transcendentals=2 * 10**6),
        name="attend",
    )(lengths, qkv, qkv, qkv)


def attend_back_kernel(first_pair, q_ref, k_ref, v_ref, probs0_ref, probs1_ref, dctx0_ref, dctx1_ref, *rest):
    grads_ref, sums_ref = rest[-2:]
    pair = pl.program_id(0) + first_pair
    if first_pair:

        @pl.when(pl.program_id(0) == 0)
        def _():
            grads_ref[...] = rest[0][...]
            sums_ref[...] = rest[1][...]

    pairs = grads_ref.shape[1] // (6 * HEAD_DIM)
    d_context = jnp.concatenate([dctx0_ref[...], dctx1_ref[...]], axis=0)
    d_context_t = d_context.T
    values_t = v_ref[...].astype(jnp.bfloat16).T
    queries_t = (q_ref[...] * SCALE).T
    d_queries, d_keys_t, d_values_t = [], [], []
    for side in range(2):
        lanes = slice(side * HEAD_DIM, (side + 1) * HEAD_DIM)
        d_probs = product(d_context[:, lanes], values_t[lanes])
        probs_b = jnp.concatenate([probs0_ref[side], probs1_ref[side]], axis=0)
        probs = probs_b.astype(jnp.float32)
        row_dot = jnp.sum(probs * d_probs, axis=1, keepdims=True)
        d_scores = (probs * (d_probs - row_dot)).astype(jnp.bfloat16)
        both = product(d_scores, jnp.concatenate(split_two(k_ref[:, lanes] * SCALE), axis=1))
        d_queries.append(both[:, :HEAD_DIM] + both[:, HEAD_DIM:])
        both = product(jnp.concatenate(split_two(queries_t[lanes]), axis=0), d_scores)
        d_keys_t.append(both[:HEAD_DIM] + both[HEAD_DIM:])
        d_values_t.append(product(d_context_t[lanes], probs_b))
    whole = (
        jnp.concatenate(d_queries, axis=1),
        jnp.concatenate(d_keys_t, axis=0).T,
        jnp.concatenate(d_values_t, axis=0).T,
    )
    for part, joined in enumerate(whole):
        at = pl.multiple_of((part * pairs + pair) * 2 * HEAD_DIM, 2 * HEAD_DIM)
        grads_ref[:, pl.ds(at, 2 * HEAD_DIM)] = joined.astype(jnp.bfloat16)
        sums_ref[:, pl.ds(at, 2 * HEAD_DIM)] = jnp.sum(joined, axis=0, keepdims=True)


def attend_back(qkv, probs, d_contexts, first_pair, count, so_far=()):
    seq_len, width3 = qkv.shape
    width = width3 // 3
    pairs = width // (2 * HEAD_DIM)

    def column(part):
        return pl.BlockSpec((seq_len, 2 * HEAD_DIM), lambda g: (0, part * pairs + first_pair + g))

    d_context = pl.BlockSpec((seq_len // 2, 2 * HEAD_DIM), lambda g: (0, first_pair + g))
    probs_chunk = pl.BlockSpec((2, seq_len // CHUNKS, seq_len), lambda g: (first_pair + g, 0, 0))
    results = [
        pl.BlockSpec((seq_len, width3), lambda g: (0, 0)),
        pl.BlockSpec((1, width3), lambda g: (0, 0)),
    ]
    return pl.pallas_call(
        functools.partial(attend_back_kernel, first_pair),
        out_shape=(
            jax.ShapeDtypeStruct((seq_len, width3), jnp.bfloat16),
            jax.ShapeDtypeStruct((1, width3), jnp.float32),
        ),
        grid=(count,),
        in_specs=[
            column(0),
            column(1),
            column(2),
            probs_chunk,
            probs_chunk,
            d_context,
            d_context,
        ]
        + results[: len(so_far)],
        out_specs=results,
        cost_estimate=pl.CostEstimate(flops=10**9, bytes_accessed=4 * 10**6, transcendentals=0),
        name="attend_back",
    )(qkv, qkv, qkv, *probs, *d_contexts, *so_far)


def partner(index, bit):
    core, x, z, yh = index & 1, (index >> 1) & 3, (index >> 3) & 3, index >> 5
    if bit == "core":
        core ^= 1
    elif bit == "xu":
        x ^= 1
    elif bit == "xv":
        x = 3 - x
    elif bit == "zu":
        z ^= 1
    elif bit == "zv":
        z = 3 - z
    else:
        yh ^= 1
    return ((yh * 4 + z) * 4 + x) * 2 + core


def swap_dp(values, bit):
    return lax.ppermute(values, "dp", [(d, partner(d, bit)) for d in range(64)])


def swap_tensor(values):
    return lax.ppermute(values, "tensor", [(0, 1), (1, 0)])


def block_order():
    me = lax.axis_index("dp")
    x, z = (me >> 1) & 3, (me >> 3) & 3
    mine = {
        "core": me & 1,
        "xu": ((x + 1) >> 1) & 1,
        "xv": x >> 1,
        "zu": ((z + 1) >> 1) & 1,
        "zv": z >> 1,
        "yh": me >> 5,
    }
    place = jnp.arange(64, dtype=jnp.int32)
    to = {bit: mine[bit] ^ ((place >> (5 - i)) & 1) for i, bit in enumerate(BITS)}
    to_x = 2 * to["xv"] + (to["xu"] ^ to["xv"])
    to_z = 2 * to["zv"] + (to["zu"] ^ to["zv"])
    return ((to["yh"] * 4 + to_z) * 4 + to_x) * 2 + to["core"]


def selection(order):
    feature = (order[:, None] * 16 + jnp.arange(16, dtype=jnp.int32)[None]).reshape(1024, 1)
    return (feature == jnp.arange(1024, dtype=jnp.int32)[None]).astype(jnp.bfloat16)


def ordered_rows(select, features):
    return product_nt(select, features).astype(jnp.bfloat16)


def side_rows(array, bits, bit, side):
    place = bits.index(bit)
    outer, inner = 2**place, 16 * 2 ** (len(bits) - place - 1)
    return array.reshape(outer, 2, inner, -1)[:, side].reshape(outer * inner, -1)


def without(bits, bit):
    return tuple(b for b in bits if b != bit)


def after(value, *others):
    return lax.optimization_barrier((value, *others))[0]


class Stream:
    def __init__(self, keep, got, bits):
        self.keep, self.got, self.bits = keep, got, bits

    def side(self, bit, side):
        kept = side_rows(self.keep, self.bits, bit, side)
        return kept if self.got is None else kept + side_rows(self.got, self.bits, bit, side)


def level(streams, bit, *before):
    if before:
        for s in streams:
            s.keep = after(s.keep, *before)
    sends = [s.side(bit, 1) for s in streams]
    keeps = [s.side(bit, 0) for s in streams]
    send = sends[0] if len(sends) == 1 else jnp.concatenate(sends, axis=1)
    got = swap_dp(send, bit)
    at = 0
    for s, keep in zip(streams, keeps):
        width = keep.shape[1]
        s.keep, s.got, s.bits = keep, got[:, at : at + width], without(s.bits, bit)
        at += width
    return send


def side_by_side(mine, other, place, axis):
    size = mine.shape[axis]
    shape = tuple(2 * n if i == axis else n for i, n in enumerate(mine.shape))
    empty = jnp.zeros(shape, jnp.float32)
    starts = [[p * size if i == axis else 0 for i in range(2)] for p in (place, 1 - place)]
    return lax.dynamic_update_slice(empty, mine, starts[0]) + lax.dynamic_update_slice(empty, other, starts[1])


def on_device(
    hidden_in,
    lengths,
    w_query,
    w_key,
    w_value,
    bias_q,
    bias_v,
    w_out,
    bias_out,
    gain1,
    shift1,
    w_in,
    bias_in,
    w_back,
    bias_back,
    gain2,
    shift2,
    out_grad,
):
    tokens = hidden_in.shape[0]
    width = w_query.shape[1]
    rows_of = [slice(c * tokens // CHUNKS, (c + 1) * tokens // CHUNKS) for c in range(CHUNKS)]

    def join(pieces):
        return jnp.concatenate(pieces, axis=0)

    order = block_order()
    select = selection(order)

    w_qkv = jnp.concatenate([w_query, w_key, w_value], axis=1)
    bias_qkv = jnp.concatenate([bias_q, jnp.zeros_like(bias_q), bias_v])
    qkv = product(hidden_in, w_qkv) + bias_qkv
    context, probs = [], []

    core, half_id = lax.axis_index("dp") & 1, lax.axis_index("tensor")
    piece = lax.dynamic_slice(w_out, (core * (width // 2), 0), (width // 2, w_out.shape[1]))
    came = swap_tensor(lax.optimization_barrier(piece.astype(jnp.float32)))
    beside = swap_dp(came, "core")
    w_other = side_by_side(came, beside, core, 0).astype(jnp.bfloat16)
    w_whole = jnp.where(
        half_id == 0, jnp.concatenate([w_out, w_other], axis=0), jnp.concatenate([w_other, w_out], axis=0)
    )
    saved, part = [], None
    for c in range(CHUNKS):
        part, chunk_probs = attend(qkv if part is None else after(qkv, part), lengths, c)
        saved.append((part, swap_tensor(part)))
        context.append(part.astype(jnp.bfloat16))
        probs.append(chunk_probs)
    context = join(context)
    hidden_rows = ordered_rows(select, after(hidden_in, part))
    middle_side, sent = [], None
    for rows, (part, got) in zip(rows_of, saved):
        if sent is not None:
            part = after(part, sent)
        whole = side_by_side(part, got, half_id, 1).astype(jnp.bfloat16)
        first = hidden_in[rows].astype(jnp.float32) + product(whole, w_whole) + bias_out
        norm1, inv1, middle = layer_norm(first, gain1, shift1)
        middle_b = middle.astype(jnp.bfloat16)
        pre_act = product(middle_b, w_in) + bias_in
        cdf = 0.5 * (1.0 + lax.erf(pre_act * 0.7071067811865476))
        act_b = (pre_act * cdf).astype(jnp.bfloat16)
        slope = cdf + pre_act * jnp.exp(-0.5 * pre_act * pre_act) * 0.3989422804014327
        act_b, slope = lax.optimization_barrier((act_b, slope))
        sent = product(act_b, w_back)
        middle_side.append((norm1, inv1, middle, middle_b, act_b, slope, sent, swap_tensor(sent)))
    act_b = join([s[4] for s in middle_side])
    middle_rows = ordered_rows(select, join([s[3] for s in middle_side]))
    second_side = []
    for rows, (norm1, inv1, middle, middle_b, _, slope, part, got) in zip(rows_of, middle_side):
        part = after(part, sent)
        second = middle + (part + got) + bias_back
        norm2, inv2, final = layer_norm(second, gain2, shift2)
        upstream = out_grad[rows].astype(jnp.float32)
        d_second = norm_back(upstream, norm2, inv2, gain2)
        sums = (
            jnp.sum(upstream * norm2, axis=0),
            jnp.sum(upstream, axis=0),
            jnp.sum(d_second, axis=0),
        )
        d_second_b = d_second.astype(jnp.bfloat16)
        d_pre = product(d_second_b, w_back.T) * slope
        d_pre_b = d_pre.astype(jnp.bfloat16)
        sent = product(d_pre_b, w_in.T)
        second_side.append(
            (final.astype(jnp.bfloat16), sums, d_second, d_second_b, d_pre_b, jnp.sum(d_pre, axis=0), sent, swap_tensor(sent))
        )
    grad_gain2, grad_shift2, grad_bias_back = (sum(s[1][i] for s in second_side) for i in range(3))
    grad_bias_in = sum(s[5] for s in second_side)
    second_rows = ordered_rows(select, after(join([s[3] for s in second_side]), sent))
    d_pre_b = join([s[4] for s in second_side])
    send_back, send_in = product(second_rows[512:], act_b), product(middle_rows[512:], d_pre_b)
    far_back, far_in = swap_dp(send_back, "core"), swap_dp(send_in, "core")

    def first_back(c, *before):
        norm1, inv1 = middle_side[c][:2]
        d_second, part, got = second_side[c][2], second_side[c][6], second_side[c][7]
        d_middle = after(d_second, *before) + (part + got)
        sums = (jnp.sum(d_middle * norm1, axis=0), jnp.sum(d_middle, axis=0))
        d_first = norm_back(d_middle, norm1, inv1, gain1)
        d_first_b = d_first.astype(jnp.bfloat16)
        d_context = product_nt(d_first_b, w_out).astype(jnp.bfloat16)
        return (d_first, d_first_b, d_context, sums + (jnp.sum(d_first, axis=0),))

    near_back = product(second_rows[:512], act_b) + far_back
    near_in = product(middle_rows[:512], d_pre_b) + far_in
    half = near_in.shape[1] // 2
    units = [
        Stream(near[:, at : at + half], None, BITS[1:]) for near in (near_back, near_in) for at in (0, half)
    ]
    sent = [level([unit], bit) for unit, bit in zip(units, ("xu", "xv", "zu", "zv"))]
    first_side = [first_back(0, *sent)]
    sent = [level([unit], bit, first_side[0][2]) for unit, bit in zip(units, ("xv", "xu", "zv", "zu"))]
    first_side.append(first_back(1, *sent))
    grad_gain1, grad_shift1, grad_bias_out = (sum(s[3][i] for s in first_side) for i in range(3))
    d_contexts = [side[2] for side in first_side]
    first_rows = ordered_rows(select, join([s[1] for s in first_side]))
    send_out = product(first_rows[512:], context)
    far_out = swap_dp(send_out, "core")
    d_contexts[0] = after(d_contexts[0], send_out)
    grads, grad_sums = attend_back(qkv, probs, d_contexts, 0, 4)
    send_qkv = product(hidden_rows[512:], grads)
    far_qkv = swap_dp(send_qkv, "core")
    sent = [level([unit], bit, send_qkv) for unit, bit in zip(units, ("zu", "zu", "xu", "xu"))]

    def input_part(c, *before):
        part = product_nt(after(grads, *before)[c * tokens // 2 : (c + 1) * tokens // 2], w_qkv)
        return part, swap_tensor(part)

    vectors = [
        grad_sums[0, :width],
        grad_sums[0, 2 * width :],
        grad_bias_out,
        grad_gain1,
        grad_shift1,
        grad_bias_in,
        grad_bias_back,
        grad_gain2,
        grad_shift2,
    ]
    widths = [v.shape[0] // 64 for v in vectors]
    packed = jnp.concatenate([v.reshape(64, -1) for v in vectors], axis=1)
    packed = jnp.pad(packed, ((0, 0), (0, 256 - packed.shape[1])))[order]
    packed = packed[:32] + swap_dp(packed[32:], "core")
    packed = jnp.pad(packed, ((0, 0), (0, 2048 - 256))).reshape(512, 128)
    near_qkv = product(after(hidden_rows, *sent)[:512], grads) + far_qkv
    attention = [Stream(near_qkv[:, i * width : (i + 1) * width], None, BITS[1:]) for i in range(3)]
    sent = [level([s], bit) for s, bit in zip(attention, ("xu", "xv", "zu"))]
    near_out = product(after(first_rows, *sent)[:512], context) + far_out
    attention.append(Stream(jnp.concatenate([near_out, packed], axis=1), None, BITS[1:]))
    sent = [level(attention[3:], "zv")]
    parts = [input_part(0, *sent)]
    sent = [parts[0][0]]
    input_grads = []

    def input_sum(*before):
        c = len(input_grads)
        part, got = parts[c]
        d_first = after(first_side[c][0], *before)
        input_grads.append(d_first + (part + got))

    parts.append(input_part(1, *sent))
    sent = [level([unit], bit, parts[1][0]) for unit, bit in zip(units, ("zv", "zv", "xv", "xv"))]
    sent = [level([s], bit, *sent) for s, bit in zip(attention, ("xv", "xu", "zv", "zu"))]
    output = join([after(s[0], *sent) for s in second_side])
    sent = level(attention[:2], "zu", *sent), level(attention[2:], "xu", *sent)
    input_sum(*sent)
    sent = level(attention[:2], "zv", *sent), level(attention[2:], "xv", *sent)
    input_sum(*sent)
    sent = level(units + attention, "yh", *sent)
    input_grad = join(input_grads)
    grad_w_back = jnp.concatenate([unit.keep + unit.got for unit in units[:2]], axis=1).T
    grad_w_in = jnp.concatenate([unit.keep + unit.got for unit in units[2:]], axis=1)
    grad_q, grad_k, grad_v, grad_o = (stream.keep + stream.got for stream in attention)
    summed = grad_o[:2, width:].reshape(-1)
    grad_o = grad_o[:, :width]
    pieces, at = [], 0
    for count in widths:
        pieces.append(summed[at : at + count])
        at += count
    head = (grad_q, grad_k, grad_v, pieces[0], pieces[1], grad_o.T, pieces[2], pieces[3], pieces[4])
    unit = (grad_w_in, pieces[5], grad_w_back, pieces[6], pieces[7], pieces[8])
    return (output, input_grad) + head + unit


def solution(mesh):
    placed = (
        P("dp", None),
        P("dp"),
        P(None, "tensor"),
        P(None, "tensor"),
        P(None, "tensor"),
        P("tensor"),
        P("tensor"),
        P("tensor", None),
        P(),
        P(),
        P(),
        P(None, "tensor"),
        P("tensor"),
        P("tensor", None),
        P(),
        P(),
        P(),
        P("dp", None),
    )
    return jax.shard_map(
        on_device,
        mesh=mesh,
        in_specs=placed,
        out_specs=(
            P("dp", None),
            P("dp", None),
            P("dp", "tensor"),
            P("dp", "tensor"),
            P("dp", "tensor"),
            P(("tensor", "dp")),
            P(("tensor", "dp")),
            P("tensor", "dp"),
            P("dp"),
            P("dp"),
            P("dp"),
            P("dp", "tensor"),
            P(("tensor", "dp")),
            P("tensor", "dp"),
            P("dp"),
            P("dp"),
            P("dp"),
        ),
        check_vma=False,
    )
```
